512 devices in a mesh: space: 8 (over z_lo, core), frame: 64 (over z_hi, x, y).
Axes of the slice: x: 4, y: 8, z: 8 (z_hi: 2, z_lo: 4; z = z_hi * 4 + z_lo), core: 2. Of those that a mesh axis runs over, the one named last changes fastest.
Arguments:
- series: bfloat16 [512, 64, 32, 128], P('frame', 'space'), may hold values from -6 to 6
- offsets: int32 [8], P('space'), may hold values from 0 to 32767
Outputs:
- smoothed: float32 [512, 64, 32, 128], P('frame', 'space')
The draws below stay inside these ranges and needn't reach their ends.
Inputs may be any that keep to these rules, and one draw needn't show every extreme that they name: `offsets`: one shift for each slab.
All inputs are finite; a program needn't handle non-finite values.
Results may differ from the reference program's by a relative error of at most 0.012.
The reference program's roundings to bfloat16 on the way count: a program that leaves them out, or rounds other values in their place, can miss the bound.
Values may be sent and summed in bfloat16 or wider, within the bound.
No kernel may reach another device: no remote copies, remote signals or barrier semaphores. Data moves between devices by JAX's collectives and lax.ppermute only.
A program may use at most 64 MiB of HBM per device.

```python
import jax
import jax.numpy as jnp
from jax import lax

F = 512
BV = 512
ITERS = 6
CY = 32
CZ = 128
VOX_G = 32768
NX = 64
N_SPACE = 8


def touch_ends(drawn, key, least, top_value):
    longest = drawn.shape.index(max(drawn.shape))
    spots = []
    for shift in (0, 1):
        where = [jax.random.randint(jax.random.fold_in(key, axis), (), 0, length) for axis, length in enumerate(drawn.shape)]
        where[longest] = (where[longest] + shift) % drawn.shape[longest]
        spots.append(tuple(where))
    return drawn.at[spots[0]].set(least).at[spots[1]].set(top_value)


def level_of(key, extent, pieces, smallest, top_value):
    def one(position, blocks):
        steps = jax.random.uniform(jax.random.fold_in(jax.random.fold_in(key, 6), position), (blocks,), jnp.float32, smallest / len(pieces), top_value / len(pieces))
        return jnp.repeat(jnp.exp(steps), extent[position] // blocks).reshape((-1,) + (1,) * (len(extent) - position - 1))

    level = one(*pieces[0])
    for cut in pieces[1:]:
        level = level * one(*cut)
    return level


def gaussian(key, dims, width, reach, shards=(), kind=jnp.bfloat16):
    factor_of = level_of(key, dims, shards, -0.22, 0.18) if shards else 1.0
    drawn = jax.random.normal(key, dims, jnp.float32) * width * factor_of
    return jnp.minimum(jnp.maximum(drawn, -reach), reach).astype(kind)


def setup_inputs(seed: int = 0) -> dict:
    key_list = jax.random.split(jax.random.key(seed), 3)
    return {
        "series": gaussian(key_list[0], (F, NX, CY, CZ), 1.0, 6.0, ((0, 64), (1, 8))),
        "offsets": touch_ends(jax.random.randint(key_list[1], (N_SPACE,), 0, VOX_G), jax.random.fold_in(key_list[1], 1), 0, VOX_G - 1).astype(jnp.int32),
    }


smooth_rate = 0.12

def shrink_block(block):
    size = block.shape[0]
    total = jnp.sum(jnp.square(block.astype(jnp.float32)))
    gram = jnp.dot(block, block.T, preferred_element_type=jnp.float32) * (size / (total + 1e-06))
    norm_gram = jnp.sqrt(jnp.sum(gram * gram))
    identity = jnp.eye(size, dtype=jnp.float32)
    shifted = (gram + identity).astype(jnp.bfloat16)
    inverse = (identity / (1.0 + norm_gram)).astype(jnp.bfloat16)
    for _ in range(ITERS):
        product = jnp.dot(shifted, inverse, preferred_element_type=jnp.float32).astype(jnp.bfloat16)
        inverse = (2.0 * inverse.astype(jnp.float32) - jnp.dot(inverse, product, preferred_element_type=jnp.float32)).astype(jnp.bfloat16)
    mixing = jnp.dot(gram.astype(jnp.bfloat16), inverse, preferred_element_type=jnp.float32).astype(jnp.bfloat16)
    result = lax.dot_general(mixing, block, (((0,), (0,)), ((), ())), preferred_element_type=jnp.float32)
    return result.astype(jnp.bfloat16)

def reference(series, offsets):
    flat = series.reshape(F, N_SPACE, VOX_G)
    positions = jnp.arange(VOX_G, dtype=jnp.int32)[None, :]
    forward_index = ((positions + offsets[:, None]) % VOX_G).astype(jnp.int32)
    rolled = jnp.take_along_axis(flat, forward_index[None], axis=2)
    blocks = rolled.reshape(F, N_SPACE * (VOX_G // BV), BV).transpose(1, 0, 2)
    shrunk = lax.map(shrink_block, blocks)
    merged = shrunk.transpose(1, 0, 2).reshape(F, N_SPACE, VOX_G)
    back_index = ((positions - offsets[:, None] + VOX_G) % VOX_G).astype(jnp.int32)
    restored = jnp.take_along_axis(merged, back_index[None], axis=2).reshape(F, NX, CY, CZ)
    padded = jnp.pad(restored.astype(jnp.float32), ((0, 0), (1, 1), (1, 1), (1, 1)))
    centre = padded[:, 1:-1, 1:-1, 1:-1]
    beside = padded[:, 2:, 1:-1, 1:-1] + padded[:, :-2, 1:-1, 1:-1]
    beside = beside + padded[:, 1:-1, 2:, 1:-1] + padded[:, 1:-1, :-2, 1:-1]
    beside = beside + padded[:, 1:-1, 1:-1, 2:] + padded[:, 1:-1, 1:-1, :-2]
    return (1.0 - 6.0 * smooth_rate) * centre + smooth_rate * beside
```

```python
import jax
import jax.numpy as jnp
from jax import lax
from jax.experimental import pallas as pl
from jax.experimental.pallas import tpu as pltpu
from jax.sharding import PartitionSpec as P
ITERS=6
RATE=0.12
F32=jnp.float32; BF=jnp.bfloat16
VM=pl.BlockSpec(memory_space=pltpu.VMEM); SM=pl.BlockSpec(memory_space=pltpu.SMEM); ANY=pl.BlockSpec(memory_space=pl.ANY)

def spread_kernel(off_ref, x_ref, o_ref, s_ref):
    sh = off_ref[0] & 511
    rr = sh >> 7
    lr = sh & 127
    for f in range(8):
        v = x_ref[f].astype(F32)
        s_ref[pl.ds(f, 256, stride=8), :] = v
    s_ref[2048:2088, :] = s_ref[0:40, :]
    lane = lax.broadcasted_iota(jnp.int32, (8,128), 1)
    keep = lane < 128 - lr
    back = (128 - lr) & 127
    def row(R):
        return pltpu.roll(s_ref[pl.ds(pl.multiple_of((rr+R)*8,8),8),:], back, 1)
    for j in range(0,64,2):
        rows=[row(4*j+i) for i in range(9)]
        o=[jnp.where(keep, rows[i], rows[i+1]) for i in range(8)]
        for c in range(4):
            o_ref[j,:,c*128:(c+1)*128]=o[c].astype(BF)
            o_ref[j+1,:,c*128:(c+1)*128]=o[4+c].astype(BF)

def spread(off,x):
    return pl.pallas_call(spread_kernel, out_shape=jax.ShapeDtypeStruct((64,8,512),BF),
        in_specs=[SM,VM], out_specs=VM, scratch_shapes=[pltpu.VMEM((2088,128),F32)], name="spread",
        cost_estimate=pl.CostEstimate(flops=1<<20,bytes_accessed=1<<20,transcendentals=0))(off,x)

def shrink_kernel(m_ref, y_ref, a_ref, g_ref, w_ref, z_ref):
    n=512
    m=m_ref[...]
    gram=lax.dot_general(m,m,(((1,),(1,)),((),())),preferred_element_type=F32)
    eye=lax.broadcasted_iota(jnp.int32,(n,n),0)==lax.broadcasted_iota(jnp.int32,(n,n),1)
    total=jnp.sum(jnp.where(eye,gram,0.0))
    g=gram*(n/(total+1e-6))
    norm=jnp.sqrt(jnp.sum(g*g))
    idn=jnp.where(eye,1.0,0.0)
    a=(g+idn).astype(BF)
    a_ref[...]=a
    g_ref[...]=g.astype(BF)
    c=(1.0/(1.0+norm)).astype(BF).astype(F32)
    w=(a.astype(F32)*c).astype(BF).astype(F32)
    z_ref[...]=(jnp.where(eye,2.0*c,0.0)-c*w).astype(BF)
    def step(_,carry):
        w_ref[...]=jnp.dot(z_ref[...],a_ref[...],preferred_element_type=F32).astype(BF)
        z=z_ref[...]
        z_ref[...]=(2.0*z.astype(F32)-jnp.dot(w_ref[...],z,preferred_element_type=F32)).astype(BF)
        return carry
    lax.fori_loop(0,ITERS-1,step,0)
    w_ref[...]=jnp.dot(z_ref[...],g_ref[...],preferred_element_type=F32).astype(BF)
    y_ref[...]=jnp.dot(w_ref[...],m_ref[...],preferred_element_type=F32).astype(BF)

def shrink(m):
    sc=[pltpu.VMEM((512,512),BF)]*4
    return pl.pallas_call(shrink_kernel,out_shape=jax.ShapeDtypeStruct((512,512),BF),in_specs=[VM],out_specs=VM,scratch_shapes=sc,name="shrink",
        cost_estimate=pl.CostEstimate(flops=13*2*512**3,bytes_accessed=1<<20,transcendentals=0))(m)

def _unshift_rows(y_ref, t_ref, lr, chunks, base):
    for j in chunks:
        v = y_ref[j].astype(F32)
        for c in range(4):
            t_ref[base + 4*j + c] = pltpu.roll(v[:, c*128:(c+1)*128], lr, 1)

def edges_kernel(off_ref, y_ref, first_ref, last_ref, t_ref):
    sh = off_ref[0] & 511
    rr = sh >> 7
    lr = sh & 127
    lane = lax.broadcasted_iota(jnp.int32, (8,128), 1)
    keep = lane >= lr
    for k,j in enumerate([63]+list(range(8))):
        v = y_ref[j].astype(F32)
        for c in range(4):
            t_ref[4*k + c] = pltpu.roll(v[:, c*128:(c+1)*128], lr, 1)
    prev = t_ref[3 - rr]
    for R in range(32):
        cur = t_ref[R + 4 - rr]
        first_ref[R] = jnp.where(keep, cur, prev).astype(BF)
        prev = cur
    for k,j in enumerate(range(55,64)):
        v = y_ref[j].astype(F32)
        for c in range(4):
            t_ref[4*k + c] = pltpu.roll(v[:, c*128:(c+1)*128], lr, 1)
    prev = t_ref[3 - rr]
    for R in range(32):
        cur = t_ref[R + 4 - rr]
        last_ref[R] = jnp.where(keep, cur, prev).astype(BF)
        prev = cur

def edges(off,y):
    s=jax.ShapeDtypeStruct((32,8,128),BF)
    return pl.pallas_call(edges_kernel,out_shape=(s,s),in_specs=[SM,VM],out_specs=(VM,VM),scratch_shapes=[pltpu.VMEM((36,8,128),F32)],name="edges",
        cost_estimate=pl.CostEstimate(flops=1<<16,bytes_accessed=1<<18,transcendentals=0))(off,y)

def inner_kernel(off_ref, y_ref, out_ref, part_ref, t_ref, u_ref, o_ref, sem):
    sh = off_ref[0] & 511
    rr = sh >> 7
    lr = sh & 127
    lane = lax.broadcasted_iota(jnp.int32, (8,128), 1)
    keep = lane >= lr
    for j in [63]+list(range(64)):
        v = y_ref[j].astype(F32)
        base = 0 if j==63 else 4
        for c in range(4):
            val = pltpu.roll(v[:, c*128:(c+1)*128], lr, 1)
            if j==63: t_ref[260-4 + c] = val
            else: t_ref[4 + 4*j + c] = val
    t_ref[0:4] = t_ref[256:260]
    prev = t_ref[3 - rr]
    for R in range(256):
        cur = t_ref[R + 4 - rr]
        u_ref[R] = jnp.where(keep, cur, prev)
        prev = cur
    lo = lane > 0
    hi = lane < 127
    for p in range(8):
        for y in range(32):
            R = p*32+y
            c = u_ref[R]
            s = jnp.where(hi, pltpu.roll(c,127,1), 0.0) + jnp.where(lo, pltpu.roll(c,1,1), 0.0)
            if y>0: s = s + u_ref[R-1]
            if y<31: s = s + u_ref[R+1]
            if p>0: s = s + u_ref[R-32]
            if p<7: s = s + u_ref[R+32]
            val = (1.0-6.0*RATE)*c + RATE*s
            if p in (0,7): part_ref[0 if p==0 else 1, :, y, :] = val
            else: o_ref[p-1, :, y, :] = val
        if p not in (0,7):
            pltpu.make_async_copy(o_ref.at[p-1], out_ref.at[:,p], sem.at[p-1]).start()
    for p in range(6):
        pltpu.make_async_copy(o_ref.at[p], out_ref.at[:,p+1], sem.at[p]).wait()

def inner(off,y):
    return pl.pallas_call(inner_kernel,out_shape=(jax.ShapeDtypeStruct((8,8,32,128),F32),jax.ShapeDtypeStruct((2,8,32,128),F32)),
        in_specs=[SM,VM],out_specs=(ANY,VM),scratch_shapes=[pltpu.VMEM((260,8,128),F32),pltpu.VMEM((256,8,128),F32),pltpu.VMEM((6,8,32,128),F32),pltpu.SemaphoreType.DMA((6,))],name="inner",
        cost_estimate=pl.CostEstimate(flops=1<<22,bytes_accessed=3<<19,transcendentals=0))(off,y)

def halo_kernel(lo_ref, hi_ref, part_ref, in_ref, out_ref, o_ref, sem):
    for k,h in ((0,lo_ref),(1,hi_ref)):
        for y in range(32):
            o_ref[k,:,y,:] = part_ref[k,:,y,:] + RATE*h[y].astype(F32)
        pltpu.make_async_copy(o_ref.at[k], out_ref.at[:,7*k], sem.at[k]).start()
    for k in range(2):
        pltpu.make_async_copy(o_ref.at[k], out_ref.at[:,7*k], sem.at[k]).wait()

def halo(lo,hi,part,out):
    return pl.pallas_call(halo_kernel,out_shape=jax.ShapeDtypeStruct((8,8,32,128),F32),in_specs=[VM,VM,VM,ANY],out_specs=ANY,
        scratch_shapes=[pltpu.VMEM((2,8,32,128),F32),pltpu.SemaphoreType.DMA((2,))],input_output_aliases={3:0},name="halo",
        cost_estimate=pl.CostEstimate(flops=1<<17,bytes_accessed=1<<19,transcendentals=0))(lo,hi,part,out)


def on_device(series, offsets):
    sent = spread(offsets, series.reshape(8, 256, 128))
    arrived = lax.all_to_all(sent, "frame", split_axis=0, concat_axis=0, tiled=True)
    shrunk = shrink(arrived.reshape(512, 512))
    back = lax.all_to_all(shrunk.reshape(64, 8, 512), "frame", split_axis=0, concat_axis=0, tiled=True)
    first, last = edges(offsets, back)
    count = lax.axis_size("space")
    up = [(i, i + 1) for i in range(count - 1)]
    down = [(j, i) for i, j in up]
    before = lax.ppermute(last, "space", up)
    after = lax.ppermute(first, "space", down)
    out, part = inner(offsets, back)
    return halo(before, after, part, out)


def solution(mesh):
    in_specs = (P("frame", "space", None, None), P("space"))
    out_specs = P("frame", "space", None, None)
    return jax.shard_map(
        on_device, mesh=mesh, in_specs=in_specs, out_specs=out_specs, check_vma=False
    )
```

```python
import jax
import jax.numpy as jnp
from jax import lax
from jax.experimental import pallas as pl
from jax.experimental.pallas import tpu as pltpu
from jax.sharding import PartitionSpec as P
ITERS=6
LIM=16<<20
GROUPS=[[(i + 60) % 64 for i in range(64)]]
RATE=0.12
F32=jnp.float32; BF=jnp.bfloat16
VM=pl.BlockSpec(memory_space=pltpu.VMEM); SM=pl.BlockSpec(memory_space=pltpu.SMEM); ANY=pl.BlockSpec(memory_space=pl.ANY)

def spread_kernel(off_ref, x_ref, o_ref, s_ref):
    sh = off_ref[0] & 511
    rr = sh >> 7
    lr = sh & 127
    for f in range(8):
        v = x_ref[f].astype(F32)
        s_ref[pl.ds(f, 256, stride=8), :] = v
    s_ref[2048:2088, :] = s_ref[0:40, :]
    lane = lax.broadcasted_iota(jnp.int32, (8,128), 1)
    keep = lane < 128 - lr
    back = (128 - lr) & 127
    def row(R):
        return pltpu.roll(s_ref[pl.ds(pl.multiple_of((rr+R)*8,8),8),:], back, 1)
    for j in range(0,64,2):
        rows=[row(4*j+i) for i in range(9)]
        o=[jnp.where(keep, rows[i], rows[i+1]) for i in range(8)]
        for c in range(4):
            o_ref[j,:,c*128:(c+1)*128]=o[c].astype(BF)
            o_ref[j+1,:,c*128:(c+1)*128]=o[4+c].astype(BF)

def spread(off,x):
    return pl.pallas_call(spread_kernel, out_shape=jax.ShapeDtypeStruct((64,8,512),BF),
        in_specs=[SM,VM], out_specs=VM, scratch_shapes=[pltpu.VMEM((2088,128),F32)], name="spread",
        compiler_params=pltpu.CompilerParams(vmem_limit_bytes=LIM),
        cost_estimate=pl.CostEstimate(flops=1<<20,bytes_accessed=1<<20,transcendentals=0))(off,x)

def shrink_kernel(m_ref, y_ref, a_ref, g_ref, w_ref, z_ref):
    n=512
    m=m_ref[...]
    gram=lax.dot_general(m,m,(((1,),(1,)),((),())),preferred_element_type=F32)
    eye=lax.broadcasted_iota(jnp.int32,(n,n),0)==lax.broadcasted_iota(jnp.int32,(n,n),1)
    total=jnp.sum(jnp.where(eye,gram,0.0))
    g=gram*(n/(total+1e-6))
    norm=jnp.sqrt(jnp.sum(g*g))
    idn=jnp.where(eye,1.0,0.0)
    a=(g+idn).astype(BF)
    a_ref[...]=a
    g_ref[...]=g.astype(BF)
    c=(1.0/(1.0+norm)).astype(BF).astype(F32)
    w=(a.astype(F32)*c).astype(BF).astype(F32)
    z_ref[...]=(jnp.where(eye,2.0*c,0.0)-c*w).astype(BF)
    def step(_,carry):
        w_ref[...]=jnp.dot(z_ref[...],a_ref[...],preferred_element_type=F32).astype(BF)
        z=z_ref[...]
        z_ref[...]=(2.0*z.astype(F32)-jnp.dot(w_ref[...],z,preferred_element_type=F32)).astype(BF)
        return carry
    lax.fori_loop(0,ITERS-1,step,0)
    w_ref[...]=jnp.dot(z_ref[...],g_ref[...],preferred_element_type=F32).astype(BF)
    y_ref[...]=jnp.dot(w_ref[...],m_ref[...],preferred_element_type=F32).astype(BF)

def shrink(m):
    sc=[pltpu.VMEM((512,512),BF)]*4
    return pl.pallas_call(shrink_kernel,out_shape=jax.ShapeDtypeStruct((512,512),BF),in_specs=[VM],out_specs=VM,scratch_shapes=sc,name="shrink",
        compiler_params=pltpu.CompilerParams(vmem_limit_bytes=LIM),
        cost_estimate=pl.CostEstimate(flops=13*2*512**3,bytes_accessed=1<<20,transcendentals=0))(m)

def _unshift_rows(y_ref, t_ref, lr, chunks, base):
    for j in chunks:
        v = y_ref[j].astype(F32)
        for c in range(4):
            t_ref[base + 4*j + c] = pltpu.roll(v[:, c*128:(c+1)*128], lr, 1)

def edges_kernel(off_ref, y_ref, first_ref, last_ref, t_ref):
    sh = off_ref[0] & 511
    rr = sh >> 7
    lr = sh & 127
    lane = lax.broadcasted_iota(jnp.int32, (8,128), 1)
    keep = lane >= lr
    for k,j in enumerate([63]+list(range(8))):
        v = y_ref[j].astype(F32)
        for c in range(4):
            t_ref[4*k + c] = pltpu.roll(v[:, c*128:(c+1)*128], lr, 1)
    prev = t_ref[3 - rr]
    for R in range(32):
        cur = t_ref[R + 4 - rr]
        first_ref[R] = jnp.where(keep, cur, prev).astype(BF)
        prev = cur
    for k,j in enumerate(range(55,64)):
        v = y_ref[j].astype(F32)
        for c in range(4):
            t_ref[4*k + c] = pltpu.roll(v[:, c*128:(c+1)*128], lr, 1)
    prev = t_ref[3 - rr]
    for R in range(32):
        cur = t_ref[R + 4 - rr]
        last_ref[R] = jnp.where(keep, cur, prev).astype(BF)
        prev = cur

def edges(off,y):
    s=jax.ShapeDtypeStruct((32,8,128),BF)
    return pl.pallas_call(edges_kernel,out_shape=(s,s),in_specs=[SM,VM],out_specs=(VM,VM),scratch_shapes=[pltpu.VMEM((36,8,128),F32)],name="edges",
        compiler_params=pltpu.CompilerParams(vmem_limit_bytes=LIM),
        cost_estimate=pl.CostEstimate(flops=1<<16,bytes_accessed=1<<18,transcendentals=0))(off,y)

def inner_kernel(off_ref, y_ref, out_ref, part_ref, t_ref, u_ref, o_ref, sem):
    sh = off_ref[0] & 511
    rr = sh >> 7
    lr = sh & 127
    lane = lax.broadcasted_iota(jnp.int32, (8,128), 1)
    keep = lane >= lr
    for j in [63]+list(range(64)):
        v = y_ref[j].astype(F32)
        base = 0 if j==63 else 4
        for c in range(4):
            val = pltpu.roll(v[:, c*128:(c+1)*128], lr, 1)
            if j==63: t_ref[260-4 + c] = val
            else: t_ref[4 + 4*j + c] = val
    t_ref[0:4] = t_ref[256:260]
    prev = t_ref[3 - rr]
    for R in range(256):
        cur = t_ref[R + 4 - rr]
        u_ref[R] = jnp.where(keep, cur, prev)
        prev = cur
    lo = lane > 0
    hi = lane < 127
    for p in range(8):
        for y in range(32):
            R = p*32+y
            c = u_ref[R]
            s = jnp.where(hi, pltpu.roll(c,127,1), 0.0) + jnp.where(lo, pltpu.roll(c,1,1), 0.0)
            if y>0: s = s + u_ref[R-1]
            if y<31: s = s + u_ref[R+1]
            if p>0: s = s + u_ref[R-32]
            if p<7: s = s + u_ref[R+32]
            val = (1.0-6.0*RATE)*c + RATE*s
            if p in (0,7): part_ref[0 if p==0 else 1, :, y, :] = val
            else: o_ref[p-1, :, y, :] = val
        if p not in (0,7):
            pltpu.make_async_copy(o_ref.at[p-1], out_ref.at[:,p], sem.at[p-1]).start()
    for p in range(6):
        pltpu.make_async_copy(o_ref.at[p], out_ref.at[:,p+1], sem.at[p]).wait()

def inner(off,y):
    return pl.pallas_call(inner_kernel,out_shape=(jax.ShapeDtypeStruct((8,8,32,128),F32),jax.ShapeDtypeStruct((2,8,32,128),F32)),
        in_specs=[SM,VM],out_specs=(ANY,VM),scratch_shapes=[pltpu.VMEM((260,8,128),F32),pltpu.VMEM((256,8,128),F32),pltpu.VMEM((6,8,32,128),F32),pltpu.SemaphoreType.DMA((6,))],name="inner",
        compiler_params=pltpu.CompilerParams(vmem_limit_bytes=LIM),
        cost_estimate=pl.CostEstimate(flops=1<<22,bytes_accessed=3<<19,transcendentals=0))(off,y)

def halo_kernel(lo_ref, hi_ref, part_ref, in_ref, out_ref, o_ref, sem):
    for k,h in ((0,lo_ref),(1,hi_ref)):
        for y in range(32):
            o_ref[k,:,y,:] = part_ref[k,:,y,:] + RATE*h[y].astype(F32)
        pltpu.make_async_copy(o_ref.at[k], out_ref.at[:,7*k], sem.at[k]).start()
    for k in range(2):
        pltpu.make_async_copy(o_ref.at[k], out_ref.at[:,7*k], sem.at[k]).wait()

def halo(lo,hi,part,out):
    return pl.pallas_call(halo_kernel,out_shape=jax.ShapeDtypeStruct((8,8,32,128),F32),in_specs=[VM,VM,VM,ANY],out_specs=ANY,
        scratch_shapes=[pltpu.VMEM((2,8,32,128),F32),pltpu.SemaphoreType.DMA((2,))],input_output_aliases={3:0},name="halo",
        compiler_params=pltpu.CompilerParams(vmem_limit_bytes=LIM),
        cost_estimate=pl.CostEstimate(flops=1<<17,bytes_accessed=1<<19,transcendentals=0))(lo,hi,part,out)


def on_device(series, offsets):
    sent = spread(offsets, series.reshape(8, 256, 128))
    arrived = lax.all_to_all(sent, "frame", split_axis=0, concat_axis=0, tiled=True, axis_index_groups=GROUPS)
    shrunk = shrink(arrived.reshape(512, 512))
    back = lax.all_to_all(shrunk.reshape(64, 8, 512), "frame", split_axis=0, concat_axis=0, tiled=True, axis_index_groups=GROUPS)
    first, last = edges(offsets, back)
    count = lax.axis_size("space")
    up = [(i, i + 1) for i in range(count - 1)]
    down = [(j, i) for i, j in up]
    before = lax.ppermute(last, "space", up)
    after = lax.ppermute(first, "space", down)
    out, part = inner(offsets, back)
    return halo(before, after, part, out)


def solution(mesh):
    in_specs = (P("frame", "space", None, None), P("space"))
    out_specs = P("frame", "space", None, None)
    return jax.shard_map(
        on_device, mesh=mesh, in_specs=in_specs, out_specs=out_specs, check_vma=False
    )
```

```python
import jax
import jax.numpy as jnp
from jax import lax
from jax.experimental import pallas as pl
from jax.experimental.pallas import tpu as pltpu
from jax.sharding import PartitionSpec as P
ITERS=6
LIM=16<<20
GROUPS=[[(i + 60) % 64 for i in range(64)]]
RATE=0.12
F32=jnp.float32; BF=jnp.bfloat16
VM=pl.BlockSpec(memory_space=pltpu.VMEM); SM=pl.BlockSpec(memory_space=pltpu.SMEM); ANY=pl.BlockSpec(memory_space=pl.ANY)

def spread_kernel(off_ref, x_ref, o_ref, s_ref):
    sh = off_ref[0] & 511
    rr = sh >> 7
    lr = sh & 127
    for f in range(8):
        v = x_ref[f].astype(F32)
        s_ref[pl.ds(f, 256, stride=8), :] = v
    s_ref[2048:2088, :] = s_ref[0:40, :]
    lane = lax.broadcasted_iota(jnp.int32, (8,128), 1)
    keep = lane < 128 - lr
    back = (128 - lr) & 127
    def row(R):
        return pltpu.roll(s_ref[pl.ds(pl.multiple_of((rr+R)*8,8),8),:], back, 1)
    for j in range(0,64,2):
        rows=[row(4*j+i) for i in range(9)]
        o=[jnp.where(keep, rows[i], rows[i+1]) for i in range(8)]
        for c in range(4):
            o_ref[j,:,c*128:(c+1)*128]=o[c].astype(BF)
            o_ref[j+1,:,c*128:(c+1)*128]=o[4+c].astype(BF)

def spread(off,x):
    return pl.pallas_call(spread_kernel, out_shape=jax.ShapeDtypeStruct((64,8,512),BF),
        in_specs=[SM,VM], out_specs=VM, scratch_shapes=[pltpu.VMEM((2088,128),F32)], name="spread",
        compiler_params=pltpu.CompilerParams(vmem_limit_bytes=LIM),
        cost_estimate=pl.CostEstimate(flops=1<<20,bytes_accessed=1<<20,transcendentals=0))(off,x)

def shrink_kernel(m_ref, y_ref, a_ref, g_ref, w_ref, z_ref, gram_ref):
    n=512
    q=128
    eye=lax.broadcasted_iota(jnp.int32,(q,q),0)==lax.broadcasted_iota(jnp.int32,(q,q),1)
    squares=jnp.zeros((8,n),F32)
    trace=jnp.zeros((8,q),F32)
    for i in range(2):
        r=slice(i*256,(i+1)*256)
        gram=lax.dot_general(m_ref[r,:],m_ref[...],(((1,),(1,)),((),())),preferred_element_type=F32)
        gram_ref[r,:]=gram
        squares=squares+jnp.sum((gram*gram).reshape(32,8,n),axis=0)
        for k in range(2):
            d=gram[k*q:(k+1)*q,(2*i+k)*q:(2*i+k+1)*q]
            trace=trace+jnp.sum(jnp.where(eye,d,0.0).reshape(16,8,q),axis=0)
    scale=n/(jnp.sum(trace)+1e-6)
    norm=scale*jnp.sqrt(jnp.sum(squares))
    c=(1.0/(1.0+norm)).astype(BF).astype(F32)
    for i in range(4):
        for j in range(4):
            at=(slice(i*q,(i+1)*q),slice(j*q,(j+1)*q))
            g=gram_ref[at]*scale
            g_ref[at]=g.astype(BF)
            a=((g+jnp.where(eye,1.0,0.0)) if i==j else g).astype(BF)
            a_ref[at]=a
            z=-c*(a.astype(F32)*c).astype(BF).astype(F32)
            if i==j: z=z+jnp.where(eye,2.0*c,0.0)
            z_ref[0,i*q:(i+1)*q,j*q:(j+1)*q]=z.astype(BF)
    for k in range(ITERS-1):
        z=z_ref[k%2]
        w_ref[...]=jnp.dot(z,a_ref[...],preferred_element_type=F32).astype(BF)
        z_ref[(k+1)%2]=(2.0*z.astype(F32)-jnp.dot(w_ref[...],z,preferred_element_type=F32)).astype(BF)
    w_ref[...]=jnp.dot(z_ref[(ITERS-1)%2],g_ref[...],preferred_element_type=F32).astype(BF)
    y_ref[...]=jnp.dot(w_ref[...],m_ref[...],preferred_element_type=F32).astype(BF)

def shrink(m):
    sc=[pltpu.VMEM((512,512),BF)]*3+[pltpu.VMEM((2,512,512),BF),pltpu.VMEM((512,512),F32)]
    return pl.pallas_call(shrink_kernel,out_shape=jax.ShapeDtypeStruct((512,512),BF),in_specs=[VM],out_specs=VM,scratch_shapes=sc,name="shrink",
        compiler_params=pltpu.CompilerParams(vmem_limit_bytes=LIM),
        cost_estimate=pl.CostEstimate(flops=13*2*512**3,bytes_accessed=1<<20,transcendentals=0))(m)

def smooth_inside(off_ref, y_ref, out_ref, part_ref, t_ref, u_ref, o_ref, sem):
    sh = off_ref[0] & 511
    rr = sh >> 7
    lr = sh & 127
    lane = lax.broadcasted_iota(jnp.int32, (8,128), 1)
    keep = lane >= lr
    for j in [63]+list(range(64)):
        v = y_ref[j].astype(F32)
        base = 0 if j==63 else 4
        for c in range(4):
            val = pltpu.roll(v[:, c*128:(c+1)*128], lr, 1)
            if j==63: t_ref[260-4 + c] = val
            else: t_ref[4 + 4*j + c] = val
    t_ref[0:4] = t_ref[256:260]
    prev = t_ref[3 - rr]
    for R in range(256):
        cur = t_ref[R + 4 - rr]
        u_ref[R] = jnp.where(keep, cur, prev)
        prev = cur
    lo = lane > 0
    hi = lane < 127
    for p in range(8):
        for y in range(32):
            R = p*32+y
            c = u_ref[R]
            s = jnp.where(hi, pltpu.roll(c,127,1), 0.0) + jnp.where(lo, pltpu.roll(c,1,1), 0.0)
            if y>0: s = s + u_ref[R-1]
            if y<31: s = s + u_ref[R+1]
            if p>0: s = s + u_ref[R-32]
            if p<7: s = s + u_ref[R+32]
            val = (1.0-6.0*RATE)*c + RATE*s
            if p in (0,7): part_ref[0 if p==0 else 1, :, y, :] = val
            else: o_ref[p-1, :, y, :] = val
        if p not in (0,7):
            pltpu.make_async_copy(o_ref.at[p-1], out_ref.at[:,p], sem.at[p-1]).start()
    for p in range(6):
        pltpu.make_async_copy(o_ref.at[p], out_ref.at[:,p+1], sem.at[p]).wait()

def inner_kernel(off_ref, y_ref, out_in, part_in, out_ref, part_ref, t_ref, u_ref, o_ref, sem):
    @pl.when((lax.axis_index("space") & 1) == 0)
    def _():
        smooth_inside(off_ref, y_ref, out_ref, part_ref, t_ref, u_ref, o_ref, sem)
    @pl.when((lax.axis_index("space") & 1) == 1)
    def _():
        part_ref[...] = part_in[...]

INNER_SCRATCH=[pltpu.VMEM((260,8,128),F32),pltpu.VMEM((256,8,128),F32),pltpu.VMEM((6,8,32,128),F32),pltpu.SemaphoreType.DMA((6,))]
INNER_SHAPE=(jax.ShapeDtypeStruct((8,8,32,128),F32),jax.ShapeDtypeStruct((2,8,32,128),F32))

def inner(off,y,out,part):
    return pl.pallas_call(inner_kernel,out_shape=INNER_SHAPE,
        in_specs=[SM,VM,ANY,VM],out_specs=(ANY,VM),scratch_shapes=INNER_SCRATCH,name="inner",input_output_aliases={2:0,3:1},
        compiler_params=pltpu.CompilerParams(vmem_limit_bytes=LIM),
        cost_estimate=pl.CostEstimate(flops=1<<22,bytes_accessed=3<<19,transcendentals=0))(off,y,out,part)

def edges_kernel(off_ref, y_ref, far_ref, near_ref, out_ref, part_ref, e_ref, t_ref, u_ref, o_ref, sem):
    sh = off_ref[0] & 511
    rr = sh >> 7
    lr = sh & 127
    odd = (lax.axis_index("space") & 1) == 1
    lane = lax.broadcasted_iota(jnp.int32, (8,128), 1)
    keep = lane >= lr
    for k,j in enumerate([63]+list(range(8))+list(range(55,64))):
        v = y_ref[j].astype(F32)
        for c in range(4):
            e_ref[4*k + c] = pltpu.roll(v[:, c*128:(c+1)*128], lr, 1)
    prev0 = e_ref[3 - rr]
    prev1 = e_ref[39 - rr]
    for R in range(32):
        cur0 = e_ref[R + 4 - rr]
        cur1 = e_ref[R + 40 - rr]
        first = jnp.where(keep, cur0, prev0)
        last = jnp.where(keep, cur1, prev1)
        near_ref[R] = jnp.where(odd, first, last).astype(BF)
        far_ref[R] = jnp.where(odd, last, first).astype(BF)
        prev0 = cur0
        prev1 = cur1
    @pl.when((lax.axis_index("space") & 1) == 1)
    def _():
        smooth_inside(off_ref, y_ref, out_ref, part_ref, t_ref, u_ref, o_ref, sem)

def edges(off,y):
    s=jax.ShapeDtypeStruct((32,8,128),BF)
    return pl.pallas_call(edges_kernel,out_shape=(s,s)+INNER_SHAPE,in_specs=[SM,VM],out_specs=(VM,VM,ANY,VM),scratch_shapes=[pltpu.VMEM((72,8,128),F32)]+INNER_SCRATCH,name="edges",
        compiler_params=pltpu.CompilerParams(vmem_limit_bytes=LIM),
        cost_estimate=pl.CostEstimate(flops=1<<22,bytes_accessed=3<<19,transcendentals=0))(off,y)

def halo_kernel(far_ref, near_ref, part_ref, in_ref, out_ref, o_ref, sem):
    odd = (lax.axis_index("space") & 1) == 1
    for k in range(2):
        for y in range(32):
            n = near_ref[y].astype(F32)
            f = far_ref[y].astype(F32)
            h = jnp.where(odd, n, f) if k == 0 else jnp.where(odd, f, n)
            o_ref[k,:,y,:] = part_ref[k,:,y,:] + RATE*h
        pltpu.make_async_copy(o_ref.at[k], out_ref.at[:,7*k], sem.at[k]).start()
    for k in range(2):
        pltpu.make_async_copy(o_ref.at[k], out_ref.at[:,7*k], sem.at[k]).wait()

def halo(lo,hi,part,out):
    return pl.pallas_call(halo_kernel,out_shape=jax.ShapeDtypeStruct((8,8,32,128),F32),in_specs=[VM,VM,VM,ANY],out_specs=ANY,
        scratch_shapes=[pltpu.VMEM((2,8,32,128),F32),pltpu.SemaphoreType.DMA((2,))],input_output_aliases={3:0},name="halo",
        compiler_params=pltpu.CompilerParams(vmem_limit_bytes=LIM),
        cost_estimate=pl.CostEstimate(flops=1<<17,bytes_accessed=1<<19,transcendentals=0))(lo,hi,part,out)


def on_device(series, offsets):
    sent = spread(offsets, series.reshape(8, 256, 128))
    arrived = lax.all_to_all(sent, "frame", split_axis=0, concat_axis=0, tiled=True, axis_index_groups=GROUPS)
    shrunk = shrink(arrived.reshape(512, 512))
    back = lax.all_to_all(shrunk.reshape(64, 8, 512), "frame", split_axis=0, concat_axis=0, tiled=True, axis_index_groups=GROUPS)
    far, near, out, part = edges(offsets, back)
    count = lax.axis_size("space")
    across = [(i, i + 1) for i in range(1, count - 1, 2)]
    far_in = lax.ppermute(far, "space", across + [(j, i) for i, j in across])
    near_in = lax.ppermute(near, "space", [(i, i ^ 1) for i in range(count)])
    out, part = inner(offsets, back, out, part)
    return halo(far_in, near_in, part, out)


def solution(mesh):
    in_specs = (P("frame", "space", None, None), P("space"))
    out_specs = P("frame", "space", None, None)
    return jax.shard_map(
        on_device, mesh=mesh, in_specs=in_specs, out_specs=out_specs, check_vma=False
    )
```

```python
import jax
import jax.numpy as jnp
from jax import lax
from jax.experimental import pallas as pl
from jax.experimental.pallas import tpu as pltpu
from jax.sharding import PartitionSpec as P
ITERS=6
LIM=16<<20
ROOT=61
def _steps(i):
    ring=lambda a,b,n: min((a-b)%n,(b-a)%n)
    return 4*(i//32 != ROOT//32) + ring(i//8%4, ROOT//8%4, 4) + ring(i%8, ROOT%8, 8)
GROUPS=[[ROOT]+sorted([i for i in range(64) if i != ROOT], key=lambda i: (-_steps(i), i))]
RATE=0.12
F32=jnp.float32; BF=jnp.bfloat16
VM=pl.BlockSpec(memory_space=pltpu.VMEM); SM=pl.BlockSpec(memory_space=pltpu.SMEM); ANY=pl.BlockSpec(memory_space=pl.ANY)

def spread_kernel(off_ref, x_ref, o_ref, s_ref):
    sh = off_ref[0] & 511
    rr = sh >> 7
    lr = sh & 127
    for f in range(8):
        v = x_ref[f].astype(F32)
        s_ref[pl.ds(f, 256, stride=8), :] = v
    s_ref[2048:2088, :] = s_ref[0:40, :]
    lane = lax.broadcasted_iota(jnp.int32, (8,128), 1)
    keep = lane < 128 - lr
    back = (128 - lr) & 127
    def row(R):
        return pltpu.roll(s_ref[pl.ds(pl.multiple_of((rr+R)*8,8),8),:], back, 1)
    for j in range(0,64,2):
        rows=[row(4*j+i) for i in range(9)]
        o=[jnp.where(keep, rows[i], rows[i+1]) for i in range(8)]
        for c in range(4):
            o_ref[j,:,c*128:(c+1)*128]=o[c].astype(BF)
            o_ref[j+1,:,c*128:(c+1)*128]=o[4+c].astype(BF)

def spread(off,x):
    return pl.pallas_call(spread_kernel, out_shape=jax.ShapeDtypeStruct((64,8,512),BF),
        in_specs=[SM,VM], out_specs=VM, scratch_shapes=[pltpu.VMEM((2088,128),F32)], name="spread",
        compiler_params=pltpu.CompilerParams(vmem_limit_bytes=LIM),
        cost_estimate=pl.CostEstimate(flops=1<<20,bytes_accessed=1<<20,transcendentals=0))(off,x)

def shrink_kernel(m_ref, y_ref, a_ref, g_ref, w_ref, z_ref, gram_ref):
    n=512
    q=128
    eye=lax.broadcasted_iota(jnp.int32,(q,q),0)==lax.broadcasted_iota(jnp.int32,(q,q),1)
    squares=jnp.zeros((8,n),F32)
    trace=jnp.zeros((8,q),F32)
    for i in range(2):
        r=slice(i*256,(i+1)*256)
        gram=lax.dot_general(m_ref[r,:],m_ref[...],(((1,),(1,)),((),())),preferred_element_type=F32)
        gram_ref[r,:]=gram
        squares=squares+jnp.sum((gram*gram).reshape(32,8,n),axis=0)
        for k in range(2):
            d=gram[k*q:(k+1)*q,(2*i+k)*q:(2*i+k+1)*q]
            trace=trace+jnp.sum(jnp.where(eye,d,0.0).reshape(16,8,q),axis=0)
    scale=n/(jnp.sum(trace)+1e-6)
    norm=scale*jnp.sqrt(jnp.sum(squares))
    c=(1.0/(1.0+norm)).astype(BF).astype(F32)
    for i in range(4):
        for j in range(4):
            at=(slice(i*q,(i+1)*q),slice(j*q,(j+1)*q))
            g=gram_ref[at]*scale
            g_ref[at]=g.astype(BF)
            a=((g+jnp.where(eye,1.0,0.0)) if i==j else g).astype(BF)
            a_ref[at]=a
            z=-c*(a.astype(F32)*c).astype(BF).astype(F32)
            if i==j: z=z+jnp.where(eye,2.0*c,0.0)
            z_ref[0,i*q:(i+1)*q,j*q:(j+1)*q]=z.astype(BF)
    for k in range(ITERS-1):
        z=z_ref[k%2]
        w_ref[...]=jnp.dot(z,a_ref[...],preferred_element_type=F32).astype(BF)
        z_ref[(k+1)%2]=(2.0*z.astype(F32)-jnp.dot(w_ref[...],z,preferred_element_type=F32)).astype(BF)
    w_ref[...]=jnp.dot(z_ref[(ITERS-1)%2],g_ref[...],preferred_element_type=F32).astype(BF)
    y_ref[...]=jnp.dot(w_ref[...],m_ref[...],preferred_element_type=F32).astype(BF)

def shrink(m):
    sc=[pltpu.VMEM((512,512),BF)]*3+[pltpu.VMEM((2,512,512),BF),pltpu.VMEM((512,512),F32)]
    return pl.pallas_call(shrink_kernel,out_shape=jax.ShapeDtypeStruct((512,512),BF),in_specs=[VM],out_specs=VM,scratch_shapes=sc,name="shrink",
        compiler_params=pltpu.CompilerParams(vmem_limit_bytes=LIM),
        cost_estimate=pl.CostEstimate(flops=13*2*512**3,bytes_accessed=1<<20,transcendentals=0))(m)

def smooth_inside(off_ref, y_ref, out_ref, part_ref, t_ref, u_ref, s_ref, o_ref, sem):
    sh = off_ref[0] & 511
    rr = sh >> 7
    lr = sh & 127
    lane = lax.broadcasted_iota(jnp.int32, (8,128), 1)
    keep = lane >= lr
    lo = lane > 0
    hi = lane < 127
    def fetch(j):
        v = y_ref[j].astype(F32)
        for c in range(4):
            val = pltpu.roll(v[:, c*128:(c+1)*128], lr, 1)
            t_ref[4 + 4*j + c] = val
            if j == 63: t_ref[c] = val
    def restore(p):
        prev = t_ref[p*32 + 3 - rr]
        for R in range(p*32, p*32+32):
            cur = t_ref[R + 4 - rr]
            u_ref[R] = jnp.where(keep, cur, prev)
            prev = cur
    fetch(63)
    for p in range(8):
        for j in range(8*p, 8*p+8):
            if j != 63: fetch(j)
        restore(p)
        if p > 0: smooth(p-1, u_ref, s_ref, o_ref, out_ref, part_ref, sem, lo, hi)
    smooth(7, u_ref, s_ref, o_ref, out_ref, part_ref, sem, lo, hi)
    for p in range(1, 7):
        pltpu.make_async_copy(o_ref.at[p-1], out_ref.at[:,p], sem.at[p-1]).wait()

def smooth(p, u_ref, s_ref, o_ref, out_ref, part_ref, sem, lo, hi):
    for y in range(32):
        R = p*32+y
        c = u_ref[R]
        s = jnp.where(hi, pltpu.roll(c,127,1), 0.0) + jnp.where(lo, pltpu.roll(c,1,1), 0.0)
        if y>0: s = s + u_ref[R-1]
        if y<31: s = s + u_ref[R+1]
        if p>0: s = s + u_ref[R-32]
        if p<7: s = s + u_ref[R+32]
        val = (1.0-6.0*RATE)*c + RATE*s
        if p in (0,7): part_ref[p//7, y*8:(y+1)*8, :] = val
        else: s_ref[R*8:(R+1)*8, :] = val
    if p not in (0,7):
        for f in range(8):
            o_ref[p-1, f] = s_ref[pl.ds(p*256+f, 32, stride=8), :]
        pltpu.make_async_copy(o_ref.at[p-1], out_ref.at[:,p], sem.at[p-1]).start()

def inner_kernel(off_ref, y_ref, out_in, part_in, out_ref, part_ref, t_ref, u_ref, s_ref, o_ref, sem):
    @pl.when((lax.axis_index("space") & 1) == 0)
    def _():
        smooth_inside(off_ref, y_ref, out_ref, part_ref, t_ref, u_ref, s_ref, o_ref, sem)
    @pl.when((lax.axis_index("space") & 1) == 1)
    def _():
        part_ref[...] = part_in[...]

INNER_SCRATCH=[pltpu.VMEM((260,8,128),F32),pltpu.VMEM((256,8,128),F32),pltpu.VMEM((2048,128),F32),pltpu.VMEM((6,8,32,128),F32),pltpu.SemaphoreType.DMA((6,))]
INNER_SHAPE=(jax.ShapeDtypeStruct((8,8,32,128),F32),jax.ShapeDtypeStruct((2,256,128),F32))

def inner(off,y,out,part):
    return pl.pallas_call(inner_kernel,out_shape=INNER_SHAPE,
        in_specs=[SM,VM,ANY,VM],out_specs=(ANY,VM),scratch_shapes=INNER_SCRATCH,name="inner",input_output_aliases={2:0,3:1},
        compiler_params=pltpu.CompilerParams(vmem_limit_bytes=LIM),
        cost_estimate=pl.CostEstimate(flops=1<<22,bytes_accessed=3<<19,transcendentals=0))(off,y,out,part)

def edges_kernel(off_ref, y_ref, far_ref, near_ref, out_ref, part_ref, e_ref, t_ref, u_ref, s_ref, o_ref, sem):
    sh = off_ref[0] & 511
    rr = sh >> 7
    lr = sh & 127
    odd = (lax.axis_index("space") & 1) == 1
    lane = lax.broadcasted_iota(jnp.int32, (8,128), 1)
    keep = lane >= lr
    for k,j in enumerate([63]+list(range(8))+list(range(55,64))):
        v = y_ref[j].astype(F32)
        for c in range(4):
            e_ref[4*k + c] = pltpu.roll(v[:, c*128:(c+1)*128], lr, 1)
    prev0 = e_ref[3 - rr]
    prev1 = e_ref[39 - rr]
    for R in range(32):
        cur0 = e_ref[R + 4 - rr]
        cur1 = e_ref[R + 40 - rr]
        first = jnp.where(keep, cur0, prev0)
        last = jnp.where(keep, cur1, prev1)
        near_ref[R] = jnp.where(odd, first, last).astype(BF)
        far_ref[R] = jnp.where(odd, last, first).astype(BF)
        prev0 = cur0
        prev1 = cur1
    @pl.when((lax.axis_index("space") & 1) == 1)
    def _():
        smooth_inside(off_ref, y_ref, out_ref, part_ref, t_ref, u_ref, s_ref, o_ref, sem)

def edges(off,y):
    s=jax.ShapeDtypeStruct((32,8,128),BF)
    return pl.pallas_call(edges_kernel,out_shape=(s,s)+INNER_SHAPE,in_specs=[SM,VM],out_specs=(VM,VM,ANY,VM),scratch_shapes=[pltpu.VMEM((72,8,128),F32)]+INNER_SCRATCH,name="edges",
        compiler_params=pltpu.CompilerParams(vmem_limit_bytes=LIM),
        cost_estimate=pl.CostEstimate(flops=1<<22,bytes_accessed=3<<19,transcendentals=0))(off,y)

def halo_kernel(far_ref, near_ref, part_ref, in_ref, out_ref, s_ref, o_ref, sem):
    odd = (lax.axis_index("space") & 1) == 1
    for k in range(2):
        for y in range(32):
            n = near_ref[y].astype(F32)
            f = far_ref[y].astype(F32)
            h = jnp.where(odd, n, f) if k == 0 else jnp.where(odd, f, n)
            s_ref[k, y*8:(y+1)*8, :] = part_ref[k, y*8:(y+1)*8, :] + RATE*h
        for f in range(8):
            o_ref[k, f] = s_ref[k, pl.ds(f, 32, stride=8), :]
        pltpu.make_async_copy(o_ref.at[k], out_ref.at[:,7*k], sem.at[k]).start()
    for k in range(2):
        pltpu.make_async_copy(o_ref.at[k], out_ref.at[:,7*k], sem.at[k]).wait()

def halo(far,near,part,out):
    return pl.pallas_call(halo_kernel,out_shape=jax.ShapeDtypeStruct((8,8,32,128),F32),in_specs=[VM,VM,VM,ANY],out_specs=ANY,
        scratch_shapes=[pltpu.VMEM((2,256,128),F32),pltpu.VMEM((2,8,32,128),F32),pltpu.SemaphoreType.DMA((2,))],input_output_aliases={3:0},name="halo",
        compiler_params=pltpu.CompilerParams(vmem_limit_bytes=LIM),
        cost_estimate=pl.CostEstimate(flops=1<<17,bytes_accessed=1<<19,transcendentals=0))(far,near,part,out)


def on_device(series, offsets):
    sent = spread(offsets, series.reshape(8, 256, 128))
    arrived = lax.all_to_all(sent, "frame", split_axis=0, concat_axis=0, tiled=True, axis_index_groups=GROUPS)
    shrunk = shrink(arrived.reshape(512, 512))
    back = lax.all_to_all(shrunk.reshape(64, 8, 512), "frame", split_axis=0, concat_axis=0, tiled=True, axis_index_groups=GROUPS)
    far, near, out, part = edges(offsets, back)
    count = lax.axis_size("space")
    across = [(i, i + 1) for i in range(1, count - 1, 2)]
    far_in = lax.ppermute(far, "space", across + [(j, i) for i, j in across])
    near_in = lax.ppermute(near, "space", [(i, i ^ 1) for i in range(count)])
    out, part = inner(offsets, back, out, part)
    return halo(far_in, near_in, part, out)


def solution(mesh):
    in_specs = (P("frame", "space", None, None), P("space"))
    out_specs = P("frame", "space", None, None)
    return jax.shard_map(
        on_device, mesh=mesh, in_specs=in_specs, out_specs=out_specs, check_vma=False
    )
```

```python
import functools
import jax
import jax.numpy as jnp
from jax import lax
from jax.experimental import pallas as pl
from jax.experimental.pallas import tpu as pltpu
from jax.sharding import PartitionSpec as P
ITERS=6
LIM=16<<20
ROOT=61
def _steps(i):
    ring=lambda a,b,n: min((a-b)%n,(b-a)%n)
    return 4*(i//32 != ROOT//32) + ring(i//8%4, ROOT//8%4, 4) + ring(i%8, ROOT%8, 8)
GROUPS=[[ROOT]+sorted([i for i in range(64) if i != ROOT], key=lambda i: (-_steps(i), i))]
RATE=0.12
F32=jnp.float32; BF=jnp.bfloat16
VM=pl.BlockSpec(memory_space=pltpu.VMEM); SM=pl.BlockSpec(memory_space=pltpu.SMEM); ANY=pl.BlockSpec(memory_space=pl.ANY)

def spread_kernel(off_ref, x_ref, o_ref, s_ref):
    sh = off_ref[0] & 511
    rr = sh >> 7
    lr = sh & 127
    for f in range(8):
        v = x_ref[f].astype(F32)
        s_ref[pl.ds(f, 256, stride=8), :] = v
    s_ref[2048:2088, :] = s_ref[0:40, :]
    lane = lax.broadcasted_iota(jnp.int32, (8,128), 1)
    keep = lane < 128 - lr
    back = (128 - lr) & 127
    def row(R):
        return pltpu.roll(s_ref[pl.ds(pl.multiple_of((rr+R)*8,8),8),:], back, 1)
    for j in range(0,64,2):
        rows=[row(4*j+i) for i in range(9)]
        o=[jnp.where(keep, rows[i], rows[i+1]) for i in range(8)]
        for c in range(4):
            o_ref[j,:,c*128:(c+1)*128]=o[c].astype(BF)
            o_ref[j+1,:,c*128:(c+1)*128]=o[4+c].astype(BF)

def spread(off,x):
    return pl.pallas_call(spread_kernel, out_shape=jax.ShapeDtypeStruct((64,8,512),BF),
        in_specs=[SM,VM], out_specs=VM, scratch_shapes=[pltpu.VMEM((2088,128),F32)], name="spread",
        compiler_params=pltpu.CompilerParams(vmem_limit_bytes=LIM),
        cost_estimate=pl.CostEstimate(flops=1<<20,bytes_accessed=1<<20,transcendentals=0))(off,x)

def shrink_kernel(m_ref, y_ref, a_ref, g_ref, w_ref, z_ref, gram_ref):
    n=512
    q=128
    eye=lax.broadcasted_iota(jnp.int32,(q,q),0)==lax.broadcasted_iota(jnp.int32,(q,q),1)
    squares=jnp.zeros((8,n),F32)
    trace=jnp.zeros((8,q),F32)
    for i in range(2):
        r=slice(i*256,(i+1)*256)
        gram=lax.dot_general(m_ref[r,:],m_ref[...],(((1,),(1,)),((),())),preferred_element_type=F32)
        gram_ref[r,:]=gram
        squares=squares+jnp.sum((gram*gram).reshape(32,8,n),axis=0)
        for k in range(2):
            d=gram[k*q:(k+1)*q,(2*i+k)*q:(2*i+k+1)*q]
            trace=trace+jnp.sum(jnp.where(eye,d,0.0).reshape(16,8,q),axis=0)
    scale=n/(jnp.sum(trace)+1e-6)
    norm=scale*jnp.sqrt(jnp.sum(squares))
    c=(1.0/(1.0+norm)).astype(BF).astype(F32)
    for i in range(4):
        for j in range(4):
            at=(slice(i*q,(i+1)*q),slice(j*q,(j+1)*q))
            g=gram_ref[at]*scale
            g_ref[at]=g.astype(BF)
            a=((g+jnp.where(eye,1.0,0.0)) if i==j else g).astype(BF)
            a_ref[at]=a
            z=-c*(a.astype(F32)*c).astype(BF).astype(F32)
            if i==j: z=z+jnp.where(eye,2.0*c,0.0)
            z_ref[0,i*q:(i+1)*q,j*q:(j+1)*q]=z.astype(BF)
    for k in range(ITERS-1):
        z=z_ref[k%2]
        w_ref[...]=jnp.dot(z,a_ref[...],preferred_element_type=F32).astype(BF)
        z_ref[(k+1)%2]=(2.0*z.astype(F32)-jnp.dot(w_ref[...],z,preferred_element_type=F32)).astype(BF)
    w_ref[...]=jnp.dot(z_ref[(ITERS-1)%2],g_ref[...],preferred_element_type=F32).astype(BF)
    y_ref[...]=jnp.dot(w_ref[...],m_ref[...],preferred_element_type=F32).astype(BF)

def shrink(m):
    sc=[pltpu.VMEM((512,512),BF)]*3+[pltpu.VMEM((2,512,512),BF),pltpu.VMEM((512,512),F32)]
    return pl.pallas_call(shrink_kernel,out_shape=jax.ShapeDtypeStruct((512,512),BF),in_specs=[VM],out_specs=VM,scratch_shapes=sc,name="shrink",
        compiler_params=pltpu.CompilerParams(vmem_limit_bytes=LIM),
        cost_estimate=pl.CostEstimate(flops=13*2*512**3,bytes_accessed=1<<20,transcendentals=0))(m)

def smooth_inside(off_ref, y_ref, out_ref, part_ref, t_ref, u_ref, s_ref, o_ref, sem):
    sh = off_ref[0] & 511
    rr = sh >> 7
    lr = sh & 127
    lane = lax.broadcasted_iota(jnp.int32, (8,128), 1)
    keep = lane >= lr
    lo = lane > 0
    hi = lane < 127
    def fetch(j):
        v = y_ref[j].astype(F32)
        for c in range(4):
            val = pltpu.roll(v[:, c*128:(c+1)*128], lr, 1)
            t_ref[4 + 4*j + c] = val
            if j == 63: t_ref[c] = val
    def restore(p):
        prev = t_ref[p*32 + 3 - rr]
        for R in range(p*32, p*32+32):
            cur = t_ref[R + 4 - rr]
            u_ref[R] = jnp.where(keep, cur, prev)
            prev = cur
    fetch(63)
    for p in range(8):
        for j in range(8*p, 8*p+8):
            if j != 63: fetch(j)
        restore(p)
        if p > 0: smooth(p-1, u_ref, s_ref, o_ref, out_ref, part_ref, sem, lo, hi)
    smooth(7, u_ref, s_ref, o_ref, out_ref, part_ref, sem, lo, hi)
    for p in range(1, 7):
        pltpu.make_async_copy(o_ref.at[p-1], out_ref.at[:,p], sem.at[p-1]).wait()

def smooth(p, u_ref, s_ref, o_ref, out_ref, part_ref, sem, lo, hi):
    for y in range(32):
        R = p*32+y
        c = u_ref[R]
        s = jnp.where(hi, pltpu.roll(c,127,1), 0.0) + jnp.where(lo, pltpu.roll(c,1,1), 0.0)
        if y>0: s = s + u_ref[R-1]
        if y<31: s = s + u_ref[R+1]
        if p>0: s = s + u_ref[R-32]
        if p<7: s = s + u_ref[R+32]
        val = (1.0-6.0*RATE)*c + RATE*s
        if p in (0,7): part_ref[p//7, y*8:(y+1)*8, :] = val
        else: s_ref[R*8:(R+1)*8, :] = val
    if p not in (0,7):
        for f in range(8):
            o_ref[p-1, f] = s_ref[pl.ds(p*256+f, 32, stride=8), :]
        pltpu.make_async_copy(o_ref.at[p-1], out_ref.at[:,p], sem.at[p-1]).start()

def inner_kernel(off_ref, y_ref, out_in, part_in, out_ref, part_ref, t_ref, u_ref, s_ref, o_ref, sem):
    @pl.when((lax.axis_index("space") & 1) == 0)
    def _():
        smooth_inside(off_ref, y_ref, out_ref, part_ref, t_ref, u_ref, s_ref, o_ref, sem)
    @pl.when((lax.axis_index("space") & 1) == 1)
    def _():
        part_ref[...] = part_in[...]

INNER_SCRATCH=[pltpu.VMEM((260,8,128),F32),pltpu.VMEM((256,8,128),F32),pltpu.VMEM((2048,128),F32),pltpu.VMEM((6,8,32,128),F32),pltpu.SemaphoreType.DMA((6,))]
INNER_SHAPE=(jax.ShapeDtypeStruct((8,8,32,128),F32),jax.ShapeDtypeStruct((2,256,128),F32))

def inner(off,y,out,part):
    return pl.pallas_call(inner_kernel,out_shape=INNER_SHAPE,
        in_specs=[SM,VM,ANY,VM],out_specs=(ANY,VM),scratch_shapes=INNER_SCRATCH,name="inner",input_output_aliases={2:0,3:1},
        compiler_params=pltpu.CompilerParams(vmem_limit_bytes=LIM),
        cost_estimate=pl.CostEstimate(flops=1<<22,bytes_accessed=3<<19,transcendentals=0))(off,y,out,part)

def edges_kernel(off_ref, y_ref, far_ref, near_ref, out_ref, part_ref, e_ref, t_ref, u_ref, s_ref, o_ref, sem):
    sh = off_ref[0] & 511
    rr = sh >> 7
    lr = sh & 127
    odd = (lax.axis_index("space") & 1) == 1
    lane = lax.broadcasted_iota(jnp.int32, (8,128), 1)
    keep = lane >= lr
    for k,j in enumerate([63]+list(range(8))+list(range(55,64))):
        v = y_ref[j].astype(F32)
        for c in range(4):
            e_ref[4*k + c] = pltpu.roll(v[:, c*128:(c+1)*128], lr, 1)
    prev0 = e_ref[3 - rr]
    prev1 = e_ref[39 - rr]
    for R in range(32):
        cur0 = e_ref[R + 4 - rr]
        cur1 = e_ref[R + 40 - rr]
        first = jnp.where(keep, cur0, prev0)
        last = jnp.where(keep, cur1, prev1)
        near_ref[R] = jnp.where(odd, first, last).astype(BF)
        far_ref[R] = jnp.where(odd, last, first).astype(BF)
        prev0 = cur0
        prev1 = cur1
    @pl.when((lax.axis_index("space") & 1) == 1)
    def _():
        smooth_inside(off_ref, y_ref, out_ref, part_ref, t_ref, u_ref, s_ref, o_ref, sem)

def edges(off,y):
    s=jax.ShapeDtypeStruct((32,8,128),BF)
    return pl.pallas_call(edges_kernel,out_shape=(s,s)+INNER_SHAPE,in_specs=[SM,VM],out_specs=(VM,VM,ANY,VM),scratch_shapes=[pltpu.VMEM((72,8,128),F32)]+INNER_SCRATCH,name="edges",
        compiler_params=pltpu.CompilerParams(vmem_limit_bytes=LIM),
        cost_estimate=pl.CostEstimate(flops=1<<22,bytes_accessed=3<<19,transcendentals=0))(off,y)

def plane_kernel(far, h_ref, part_ref, in_ref, out_ref, s_ref, o_ref, sem):
    odd = lax.axis_index("space") & 1
    k = odd if far else 1 - odd
    for y in range(32):
        s_ref[y*8:(y+1)*8, :] = part_ref[k, y*8:(y+1)*8, :] + RATE*h_ref[y].astype(F32)
    for f in range(8):
        o_ref[f] = s_ref[pl.ds(f, 32, stride=8), :]
    copy = pltpu.make_async_copy(o_ref, out_ref.at[:, 7*k], sem)
    copy.start()
    copy.wait()

def add_plane(far,h,part,out):
    return pl.pallas_call(functools.partial(plane_kernel,far),out_shape=jax.ShapeDtypeStruct((8,8,32,128),F32),in_specs=[VM,VM,ANY],out_specs=ANY,
        scratch_shapes=[pltpu.VMEM((256,128),F32),pltpu.VMEM((8,32,128),F32),pltpu.SemaphoreType.DMA],input_output_aliases={2:0},name="far_plane" if far else "near_plane",
        compiler_params=pltpu.CompilerParams(vmem_limit_bytes=LIM),
        cost_estimate=pl.CostEstimate(flops=1<<16,bytes_accessed=1<<18,transcendentals=0))(h,part,out)


def on_device(series, offsets):
    sent = spread(offsets, series.reshape(8, 256, 128))
    arrived = lax.all_to_all(sent, "frame", split_axis=0, concat_axis=0, tiled=True, axis_index_groups=GROUPS)
    shrunk = shrink(arrived.reshape(512, 512))
    back = lax.all_to_all(shrunk.reshape(64, 8, 512), "frame", split_axis=0, concat_axis=0, tiled=True, axis_index_groups=GROUPS)
    far, near, out, part = edges(offsets, back)
    count = lax.axis_size("space")
    across = [(i, i + 1) for i in range(1, count - 1, 2)]
    far_in = lax.ppermute(far, "space", across + [(j, i) for i, j in across])
    out, part = inner(offsets, back, out, part)
    near, part = lax.optimization_barrier((near, part))
    near_in = lax.ppermute(near, "space", [(i, i ^ 1) for i in range(count)])
    out = add_plane(True, far_in, part, out)
    return add_plane(False, near_in, part, out)


def solution(mesh):
    in_specs = (P("frame", "space", None, None), P("space"))
    out_specs = P("frame", "space", None, None)
    return jax.shard_map(
        on_device, mesh=mesh, in_specs=in_specs, out_specs=out_specs, check_vma=False
    )
```
